32 devices in a mesh: dom: 32 (over z, y, x, core).
Axes of the slice: x: 2, y: 2, z: 4, core: 2. Of those that a mesh axis runs over, the one named last changes fastest.
Arguments:
- rhs: float32 [128, 12, 512], P('dom'), may hold values from -18 to 18
- stiffness: float32 [512, 512], replicated, may hold values from -0.25 to 0.25
- vol_jac: float32 [128, 12, 12], P('dom'), may hold values from -0.9 to 0.9
- face_jac: float32 [128, 6, 12, 12], P('dom'), may hold values from -1.5 to 1.5
- block_inv: float32 [128, 12, 12, 512], P('dom'), as said below
- face_owner: int32 [128, 6], P('dom'), may hold values from -1 to 31, as said below
- face_elem: int32 [128, 6], P('dom'), may hold values from 0 to 3
- face_side: int32 [128, 6], P('dom'), may hold values from 0 to 5
- face_turn: int32 [128, 6], P('dom'), may hold values from 0 to 7
Outputs:
- correction: float32 [128, 12, 512], P('dom')
The draws below stay inside these ranges and needn't reach their ends.
Inputs may be any that keep to these rules, and one draw needn't show every extreme that they name: `face_owner`: -1 marks a face with no neighbour; any other value is the element's own partition or one next to it along the axis; of the faces of one partition exactly 8 name the partition below and exactly 8 the partition above, where that partition exists. Each block_inv[e, :, :, m] is a full 12 x 12 matrix.
All inputs are finite; a program needn't handle non-finite values.
Results may differ from the reference program's by a relative error of at most 0.0001.
Values sent between devices are 32-bit elements; how exact they have to be, the bound alone decides.
A program may use at most 64 MiB of HBM per device.

```python
import jax
import jax.numpy as jnp
from jax import lax

VARS = 12
QF = 8
QC = 4
E_DEV = 4
MODES = 512
ELEMS = 128


def draw_block_inv(key, part):
    first_key, second_key = jax.random.split(jax.random.fold_in(key, 11))
    diagonal = jnp.exp(jax.random.uniform(first_key, (ELEMS, VARS, MODES), jnp.float32, jnp.log(0.2), jnp.log(0.5)))
    spread = 0.05 * jax.random.normal(second_key, (ELEMS, VARS, VARS, MODES), jnp.float32)
    identity = (jnp.arange(VARS)[:, None] == jnp.arange(VARS)[None, :]).astype(jnp.float32)[:, :, None]
    return spread * (1.0 - identity) + identity * diagonal[:, :, None, :]


def draw_face_owner(key, part):
    first_key, second_key = jax.random.split(jax.random.fold_in(key, 23))
    partitions = ELEMS // E_DEV
    face_count = 6 * E_DEV
    part_keys = jax.random.split(first_key, partitions)
    orders = jax.vmap(lambda single: jax.random.permutation(single, face_count))(part_keys)
    offset = jnp.where(orders < 2 * E_DEV, -1, jnp.where(orders < 4 * E_DEV, 1, 0)).astype(jnp.int32).reshape(ELEMS, 6)
    dropped = (jax.random.randint(second_key, (ELEMS, 6), 0, 8, jnp.int32) == 0) & (offset == 0)
    home_part = (jnp.arange(ELEMS, dtype=jnp.int32) // E_DEV)[:, None]
    owner = home_part + offset
    outside = dropped | (owner < 0) | (owner >= partitions)
    return jnp.where(outside, -1, owner).astype(jnp.int32)


def touch_ends(result, key, low, largest):
    longest = result.shape.index(max(result.shape))
    spots = []
    for shift in (0, 1):
        where = [jax.random.randint(jax.random.fold_in(key, axis), (), 0, length) for axis, length in enumerate(result.shape)]
        where[longest] = (where[longest] + shift) % result.shape[longest]
        spots.append(tuple(where))
    return result.at[spots[0]].set(low).at[spots[1]].set(largest)


def block_scale(key, shape, cuts, least, top_value):
    factor_of = 1.0
    for axis_at, blocks in cuts:
        steps = jax.random.uniform(jax.random.fold_in(jax.random.fold_in(key, 6), axis_at), (blocks,), jnp.float32, least / len(cuts), top_value / len(cuts))
        factor_of = factor_of * jnp.repeat(jnp.exp(steps), shape[axis_at] // blocks).reshape((-1,) + (1,) * (len(shape) - 1 - axis_at))
    return factor_of


def scatter_about(own_key, extent, width, most, cuts=(), kind=jnp.bfloat16):
    result = width * jax.random.normal(own_key, extent, jnp.float32)
    if cuts:
        result = result * block_scale(own_key, extent, cuts, -0.22, 0.18)
    return jnp.clip(result, -most, most).astype(kind)


def setup_inputs(seed: int = 0) -> dict:
    key_list = jax.random.split(jax.random.key(seed), 10)
    rhs = scatter_about(key_list[0], (ELEMS, VARS, MODES), 3.0, 18.0, ((0, 32),), jnp.float32)
    stiffness = scatter_about(key_list[1], (MODES, MODES), MODES ** -0.5, 0.25, (), jnp.float32)
    vol_jac = scatter_about(key_list[2], (ELEMS, VARS, VARS), 0.15, 0.9, ((0, 32),), jnp.float32)
    face_jac = scatter_about(key_list[3], (ELEMS, 6, VARS, VARS), 0.25, 1.5, ((0, 32),), jnp.float32)
    block_inv = draw_block_inv(jax.random.fold_in(key_list[9], 71), 0)
    face_owner = draw_face_owner(jax.random.fold_in(key_list[9], 71), 0)
    face_elem = touch_ends(jax.random.randint(key_list[6], (ELEMS, 6), 0, E_DEV), jax.random.fold_in(key_list[6], 1), 0, E_DEV - 1).astype(jnp.int32)
    face_side = touch_ends(jax.random.randint(key_list[7], (ELEMS, 6), 0, 6), jax.random.fold_in(key_list[7], 1), 0, 5).astype(jnp.int32)
    face_turn = touch_ends(jax.random.randint(key_list[8], (ELEMS, 6), 0, 8), jax.random.fold_in(key_list[8], 1), 0, 7).astype(jnp.int32)
    return {"rhs": rhs, "stiffness": stiffness, "vol_jac": vol_jac, "face_jac": face_jac, "block_inv": block_inv, "face_owner": face_owner, "face_elem": face_elem, "face_side": face_side, "face_turn": face_turn}


PRECISE = lax.Precision.HIGHEST
SIGMA = 2.0
OMEGA = 0.7


def alternate(degree_count):
    return jnp.where(jnp.arange(degree_count) % 2 == 1, -1.0, 1.0).astype(jnp.float32)


def orient_faces(values, turning):
    degree_count = values.shape[-1]
    flipped = jnp.where((turning % 2 == 1)[:, None, None, None], jnp.swapaxes(values, -1, -2), values)
    signs = alternate(degree_count)
    first_sign = jnp.where(((turning // 2) % 2 == 1)[:, None], signs[None, :], 1.0)
    second_sign = jnp.where(((turning // 4) % 2 == 1)[:, None], signs[None, :], 1.0)
    return flipped * first_sign[:, None, :, None] * second_sign[:, None, None, :]


def apply_operator(iterate, vol_jac, face_jac, kernel, face_owner, face_elem, face_side, face_turn, degree_count):
    elements, variables, mode_count = iterate.shape
    cubed = iterate.reshape(elements, variables, degree_count, degree_count, degree_count)
    einsum_forms = ("evijk,i->evjk", "evijk,j->evik", "evijk,k->evij")
    degree = jnp.arange(degree_count).astype(jnp.float32)
    weight_list = []
    traces = []
    for face_id in range(6):
        if face_id % 2 == 0:
            weight_vec = alternate(degree_count)
        else:
            weight_vec = jnp.ones((degree_count,), jnp.float32)
        weight_list.append(weight_vec)
        traces.append(jnp.einsum(einsum_forms[face_id // 2], cubed, weight_vec, precision=PRECISE))
    trace_all = jnp.stack(traces, axis=1)
    present = face_owner >= 0
    slot_ids = jnp.clip(face_owner * (E_DEV * 6) + face_elem * 6 + face_side, 0, elements * 6 - 1).astype(jnp.int32)
    outside = trace_all.reshape(elements * 6, variables, degree_count, degree_count)[slot_ids.reshape(-1)]
    outside = orient_faces(outside, face_turn.reshape(-1)).reshape(elements, 6, variables, degree_count, degree_count)
    outside = outside * present.astype(jnp.float32)[:, :, None, None, None]
    jumps = jnp.einsum("efvw,efwab->efvab", face_jac, trace_all - outside, precision=PRECISE)
    lifted = jnp.zeros(cubed.shape, jnp.float32)
    for face_id in range(6):
        lift_coef = (2.0 * degree + 1.0) / 16.0 * weight_list[face_id]
        sheet_vals = jumps[:, face_id]
        normal_axis = face_id // 2
        if normal_axis == 0:
            lifted = lifted + sheet_vals[:, :, None, :, :] * lift_coef[:, None, None]
        elif normal_axis == 1:
            lifted = lifted + sheet_vals[:, :, :, None, :] * lift_coef[:, None]
        else:
            lifted = lifted + sheet_vals[:, :, :, :, None] * lift_coef
    blended = jnp.dot(iterate.reshape(elements * variables, mode_count), kernel, precision=PRECISE)
    volume = jnp.einsum("evw,ewm->evm", vol_jac, blended.reshape(elements, variables, mode_count), precision=PRECISE)
    return SIGMA * iterate + volume + lifted.reshape(elements, variables, mode_count)


def shrink(values):
    leading = values.shape[:-1]
    cubed = values.reshape(leading + (QF, QF, QF))[..., :QC, :QC, :QC]
    return cubed.reshape(leading + (QC * QC * QC,))


def widen(values):
    leading = values.shape[:-1]
    cubed = values.reshape(leading + (QC, QC, QC))
    padding = tuple((0, 0) for level in leading) + ((0, QF - QC), (0, QF - QC), (0, QF - QC))
    return jnp.pad(cubed, padding).reshape(leading + (QF * QF * QF,))


def precondition(inverse, residual):
    return jnp.einsum("evwm,ewm->evm", inverse, residual, precision=PRECISE)


def reference(rhs, stiffness, vol_jac, face_jac, block_inv, face_owner, face_elem, face_side, face_turn):
    def fine_apply(iterate):
        return apply_operator(iterate, vol_jac, face_jac, stiffness, face_owner, face_elem, face_side, face_turn, QF)

    coarse_mat = shrink(shrink(stiffness).T).T

    def coarse_apply(iterate):
        return apply_operator(iterate, vol_jac, face_jac, coarse_mat, face_owner, face_elem, face_side, face_turn, QC)

    iterate = OMEGA * precondition(block_inv, rhs)
    iterate = iterate + OMEGA * precondition(block_inv, rhs - fine_apply(iterate))
    coarse_rhs = shrink(rhs - fine_apply(iterate))
    coarse_inv = shrink(block_inv)
    sweep_one = OMEGA * precondition(coarse_inv, coarse_rhs)
    sweep_two = sweep_one + OMEGA * precondition(coarse_inv, coarse_rhs - coarse_apply(sweep_one))
    iterate = iterate + widen(sweep_two)
    for sweep in range(2):
        iterate = iterate + OMEGA * precondition(block_inv, rhs - fine_apply(iterate))
    return iterate
```

```python
import functools

import jax
import jax.numpy as jnp
import numpy as np
from jax import lax
from jax.experimental import pallas as pl
from jax.experimental.pallas import tpu as pltpu
from jax.sharding import PartitionSpec as P

QF = 8
QC = 4
SIGMA = 2.0
OMEGA = 0.7
SPAN = QF * QF
STEPS = 5
MESH = pl.DeviceIdType.MESH


def split_index(mode_id):
    return (mode_id // (QF * QF), mode_id // QF % QF, mode_id % QF)


def trace_table():
    matrix = np.zeros((QF**3, 6 * 2 * SPAN), np.float32)
    for mode_id in range(QF**3):
        triple = split_index(mode_id)
        for face_id in range(6):
            axis = face_id // 2
            a, b = [triple[place] for place in range(3) if place != axis]
            sign = (-1.0) ** triple[axis] if face_id % 2 == 0 else 1.0
            plain, turned = a * QF + b, b * QF + a
            low, high = (plain, turned) if face_id % 2 == 0 else (turned, plain)
            matrix[mode_id, face_id * 2 * SPAN + low] = sign
            matrix[mode_id, face_id * 2 * SPAN + SPAN + high] = sign
    return matrix


def lift_table():
    matrix = np.zeros((6 * SPAN, QF**3), np.float32)
    for mode_id in range(QF**3):
        triple = split_index(mode_id)
        for face_id in range(6):
            axis = face_id // 2
            a, b = [triple[place] for place in range(3) if place != axis]
            sign = (-1.0) ** triple[axis] if face_id % 2 == 0 else 1.0
            matrix[face_id * SPAN + a * QF + b, mode_id] = (2.0 * triple[axis] + 1.0) / 16.0 * sign
    return matrix


def sign_table():
    matrix = np.zeros((17, 16, 2 * SPAN), np.float32)
    for odd in range(2):
        for turn in range(8):
            half = (turn % 2) ^ odd
            for a in range(QF):
                for b in range(QF):
                    sign = 1.0
                    if turn // 2 % 2 == 1:
                        sign *= (-1.0) ** a
                    if turn // 4 % 2 == 1:
                        sign *= (-1.0) ** b
                    matrix[turn + 8 * odd, :, half * SPAN + a * QF + b] = sign
    return matrix


def low_mask():
    mask = np.zeros((8, QF**3), np.float32)
    for mode_id in range(QF**3):
        if max(split_index(mode_id)) < QC:
            mask[:, mode_id] = 1.0
    return mask


def halves(value):
    high = value.astype(jnp.bfloat16)
    return high, (value - high.astype(jnp.float32)).astype(jnp.bfloat16)


def kernel(
    n, elements, variables,
    owner, elem, side_of, turn, rhs, vol, face, signs, mask, inv_hbm, trace_hbm, stiff_hbm, lift_hbm,
    out,
    inv, inv_raw, trace, stiff, lift, stiff_hi, stiff_lo, jac_wide, vol_wide, small, jump, table,
    meta, request, asked, asked_s, base_ref, now_ref, work_ref, kept_ref, coarse_ref, fine_ref,
    sent, got0, got1, got2, got3, got4,
    load_sem, ask_send, ask_recv, ask_local, send_sem, recv_sem,
):
    got = (got0, got1, got2, got3, got4)
    me = lax.axis_index("dom")
    has = (me > 0, me < n - 1)
    other = (jnp.maximum(me - 1, 0), jnp.minimum(me + 1, n - 1))
    modes = rhs.shape[2]
    rows = elements * variables
    pairs = rows // 8
    half_reach = elements

    loads = []
    for at, (source, target) in enumerate(
        ((inv_hbm, inv_raw), (trace_hbm, trace), (stiff_hbm, stiff), (lift_hbm, lift))
    ):
        loads.append(pltpu.make_async_copy(source, target, load_sem.at[at]))
        loads[-1].start()

    barrier = pltpu.get_barrier_semaphore()
    for side in range(2):
        @pl.when(has[side])
        def _():
            pl.semaphore_signal(barrier, inc=1, device_id=(other[side],), device_id_type=MESH)

    spots = lax.broadcasted_iota(jnp.int32, (1, 128), 1)
    wanted = [jnp.zeros((1, 128), jnp.int32), jnp.zeros((1, 128), jnp.int32)]
    ranks = [jnp.int32(0), jnp.int32(0)]
    for e in range(elements):
        for f in range(6):
            at = e * 6 + f
            home = owner[e, f]
            face_turn, face_side, face_elem = turn[e, f], side_of[e, f], elem[e, f]
            present = home >= 0
            odd = face_side % 2
            swap = face_turn % 2
            half = (odd + swap) % 2
            tests = (present & (home == me - 1), present & (home == me + 1))
            for side in range(2):
                value = (face_elem * 6 + face_side) * 2 + half
                wanted[side] = jnp.where((spots == ranks[side]) & tests[side], value, wanted[side])
            rank = jnp.where(tests[1], ranks[1], ranks[0])
            far = tests[0] | tests[1]
            far_half = rank // half_reach
            meta[0, at] = jnp.where(tests[1], 1, 0)
            meta[1, at] = jnp.minimum(rank % half_reach, half_reach - 1)
            meta[2, at] = jnp.where(far, 1, 0)
            sign_row = face_turn + 8 * jnp.where(far, (far_half + swap) % 2, odd)
            meta[3, at] = jnp.where(present, sign_row, 16)
            for side in range(2):
                ranks[side] = ranks[side] + jnp.where(tests[side], 1, 0)
    request[0:1, :] = wanted[0]
    request[1:2, :] = wanted[1]

    pl.semaphore_wait(barrier, jnp.where(me > 0, 1, 0) + jnp.where(me < n - 1, 1, 0))

    def ask(side, slot):
        return pltpu.make_async_remote_copy(
            src_ref=request, dst_ref=asked.at[slot], send_sem=ask_send.at[side],
            recv_sem=ask_recv.at[slot], device_id=(other[side],), device_id_type=MESH,
        )

    for side in range(2):
        @pl.when(has[side])
        def _():
            ask(side, 1 - side).start()

    def twice(ref, w, lanes):
        row = ref[elements * w : elements * (w + 1), lanes]
        return jnp.concatenate([row, row], axis=0)

    def contract(wide, wide_lanes, source, c):
        lanes = slice(c * 128, (c + 1) * 128)
        totals = [None] * pairs
        for w in range(variables):
            row = twice(source, w, lanes)
            for p in range(pairs):
                term = wide[w, 8 * p : 8 * p + 8, wide_lanes] * row
                totals[p] = term if totals[p] is None else totals[p] + term
        return totals

    def smooth(source, width, emit):
        for c in range(width // 128):
            lanes = slice(c * 128, (c + 1) * 128)
            for p, total in enumerate(contract(inv, lanes, source, c)):
                emit(slice(8 * p, 8 * p + 8), lanes, OMEGA * total)

    for v in range(variables):
        base_ref[elements * v : elements * (v + 1), :] = rhs[v]
    loads[0].wait()
    for v in range(variables):
        for w in range(variables):
            inv[w, elements * v : elements * (v + 1), :] = inv_raw[v, w]

    def first(at, lanes, value):
        now_ref[at, lanes] = value

    def following(at, lanes, value):
        now_ref[at, lanes] = now_ref[at, lanes] + value

    smooth(base_ref, modes, first)

    for side in range(2):
        @pl.when(has[side])
        def _():
            ask(side, side).wait()
            copy = pltpu.make_async_copy(asked.at[side], asked_s.at[side], ask_local.at[side])
            copy.start()
            copy.wait()

    lane = lax.broadcasted_iota(jnp.int32, (variables, 2 * SPAN), 1)
    in_low = lane < SPAN

    def put(step, side, slot):
        return pltpu.make_async_remote_copy(
            src_ref=sent.at[step, side], dst_ref=got[step].at[slot], send_sem=send_sem.at[step, side],
            recv_sem=recv_sem.at[step, slot], device_id=(other[side],), device_id_type=MESH,
        )

    def face_load(place):
        return table[place % 6, pl.ds(place // 6, variables, stride=elements), :]

    def widen_jacobians():
        for f in range(6):
            for v in range(variables):
                small[f, elements * v : elements * (v + 1), :] = face[f, v]
        for v in range(variables):
            small[6, elements * v : elements * (v + 1), :] = vol[v]
        low8 = lax.broadcasted_iota(jnp.int32, (rows, 2 * SPAN), 1) < SPAN
        for w in range(variables):
            vol_wide[w] = jnp.broadcast_to(small[6, :, w : w + 1], (rows, 2 * SPAN))
            for pair in range(3):
                one = jnp.broadcast_to(small[2 * pair, :, w : w + 1], (rows, 2 * SPAN))
                two = jnp.broadcast_to(small[2 * pair + 1, :, w : w + 1], (rows, 2 * SPAN))
                jac_wide[w, :, pair * 2 * SPAN : (pair + 1) * 2 * SPAN] = jnp.where(low8, one, two)

    def residual(step, base, width_in, width_out, emit):
        value = now_ref[:, :width_in]
        high, low = halves(value)
        both = jnp.concatenate([high, low], axis=0)
        if step == 0:
            loads[1].wait()
        traced = jnp.dot(both, trace[:width_in, :], preferred_element_type=jnp.float32)
        traced = traced[:rows] + traced[rows:]
        for f in range(6):
            table[f] = traced[:, f * 2 * SPAN : (f + 1) * 2 * SPAN]
        for side in range(2):
            @pl.when(has[side])
            def _():
                for j in range(half_reach):
                    found = []
                    for half in range(2):
                        code = jnp.clip(asked_s[side, 1 - side, half * half_reach + j], 0, 12 * elements - 1)
                        piece = face_load(code // 2)
                        found.append(jnp.where(code % 2 == half, piece, pltpu.roll(piece, SPAN, axis=1)))
                    sent[step, side, j] = jnp.where(in_low, found[0], found[1])
                put(step, side, 1 - side).start()
        if step == 0:
            loads[2].wait()
            stiff_high, stiff_low = halves(stiff[...])
            stiff_hi[...] = stiff_high
            stiff_lo[...] = stiff_low
            widen_jacobians()
        blended = jnp.dot(both, stiff_hi[:width_in, :width_out], preferred_element_type=jnp.float32)
        blended = blended[:rows] + blended[rows:]
        blended = blended + jnp.dot(high, stiff_lo[:width_in, :width_out], preferred_element_type=jnp.float32)
        work_ref[:, :width_out] = blended
        for c in range(width_out // 128):
            lanes = slice(c * 128, (c + 1) * 128)
            for p, total in enumerate(contract(vol_wide, slice(0, 128), work_ref, c)):
                at = slice(8 * p, 8 * p + 8)
                kept_ref[at, lanes] = base[at, lanes] - SIGMA * now_ref[at, lanes] - total
        for side in range(2):
            @pl.when(has[side])
            def _():
                put(step, side, side).wait()
        if step == 0:
            loads[3].wait()
        for e in range(elements):
            for pair in range(3):
                faces = []
                for f in (2 * pair, 2 * pair + 1):
                    at = e * 6 + f
                    own = face_load(elem[e, f] * 6 + side_of[e, f])
                    far = got[step][meta[0, at], meta[1, at]]
                    picked = jnp.where(meta[2, at] > 0, far, own)
                    picked = picked * signs[meta[3, at]][:variables]
                    faces.append(picked + pltpu.roll(picked, SPAN, axis=1))
                at_e = pl.ds(e, variables, stride=elements)
                mine = jnp.where(in_low, table[2 * pair, at_e, :], table[2 * pair + 1, at_e, :])
                theirs = jnp.where(in_low, faces[0], faces[1])
                jump[pair, at_e, :] = mine - theirs
        columns = []
        for pair in range(3):
            lanes = slice(pair * 128, (pair + 1) * 128)
            columns.append(jnp.concatenate(contract(jac_wide, lanes, jump.at[pair], 0), axis=0))
        flux_high, flux_low = halves(jnp.concatenate(columns, axis=1))
        lifted = jnp.dot(
            jnp.concatenate([flux_high, flux_low], axis=0), lift[:, :width_out],
            preferred_element_type=jnp.float32,
        )
        emit(kept_ref[:, :width_out] - (lifted[:rows] + lifted[rows:]))

    short = QC * SPAN
    low_of = jnp.concatenate([mask[:, :short]] * pairs, axis=0)

    def to_work(value):
        work_ref[...] = value

    def to_coarse(value):
        coarse_ref[:, :short] = value * low_of

    def to_low_work(value):
        work_ref[:, :short] = value * low_of

    residual(0, base_ref, modes, modes, to_work)
    smooth(work_ref, modes, following)
    residual(1, base_ref, modes, short, to_coarse)
    fine_ref[...] = now_ref[...]
    smooth(coarse_ref, short, first)
    residual(2, coarse_ref, short, short, to_low_work)
    smooth(work_ref, short, following)
    now_ref[:, :short] = now_ref[:, :short] + fine_ref[:, :short]
    for step in (3, 4):
        residual(step, base_ref, modes, modes, to_work)
        smooth(work_ref, modes, following)
    for v in range(variables):
        out[v] = now_ref[elements * v : elements * (v + 1), :]


def local(n, rhs, stiffness, vol_jac, face_jac, block_inv, face_owner, face_elem, face_side, face_turn):
    elements, variables, modes = rhs.shape
    reach = 2 * elements
    trace = jnp.asarray(trace_table(), jnp.bfloat16)
    lift = jnp.asarray(lift_table(), jnp.bfloat16)
    rows = elements * variables
    vmem = pl.BlockSpec(memory_space=pltpu.VMEM)
    smem = pl.BlockSpec(memory_space=pltpu.SMEM)
    hbm = pl.BlockSpec(memory_space=pl.ANY)
    f32, bf16, i32 = jnp.float32, jnp.bfloat16, jnp.int32
    dma = pltpu.SemaphoreType.DMA
    state = pltpu.VMEM((rows, modes), f32)
    result = pl.pallas_call(
        functools.partial(kernel, n, elements, variables),
        out_shape=jax.ShapeDtypeStruct((variables, elements, modes), f32),
        in_specs=[smem] * 4 + [vmem] * 5 + [hbm] * 4,
        out_specs=vmem,
        scratch_shapes=[
            pltpu.VMEM((variables, rows, modes), f32),
            pltpu.VMEM((variables, variables, elements, modes), f32),
            pltpu.VMEM(trace.shape, bf16),
            pltpu.VMEM(stiffness.shape, f32),
            pltpu.VMEM(lift.shape, bf16),
            pltpu.VMEM(stiffness.shape, bf16),
            pltpu.VMEM(stiffness.shape, bf16),
            pltpu.VMEM((variables, rows, 6 * SPAN), f32),
            pltpu.VMEM((variables, rows, 2 * SPAN), f32),
            pltpu.VMEM((7, rows, variables), f32),
            pltpu.VMEM((3, rows, 2 * SPAN), f32),
            pltpu.VMEM((6, rows, 2 * SPAN), f32),
            pltpu.SMEM((4, 6 * elements), i32),
            pltpu.VMEM((8, 128), i32),
            pltpu.VMEM((2, 8, 128), i32),
            pltpu.SMEM((2, 8, 128), i32),
            state, state, state, state, state, state,
            pltpu.VMEM((STEPS, 2, elements, variables, 2 * SPAN), f32),
        ] + [pltpu.VMEM((2, elements, variables, 2 * SPAN), f32)] * STEPS + [
            dma((4,)),
            dma((2,)),
            dma((2,)),
            dma((2,)),
            dma((STEPS, 2)),
            dma((STEPS, 2)),
        ],
        compiler_params=pltpu.CompilerParams(
            collective_id=0, has_side_effects=True, vmem_limit_bytes=60 * 1024 * 1024
        ),
    )(
        face_owner, face_elem, face_side, face_turn,
        rhs.transpose(1, 0, 2), vol_jac.transpose(1, 0, 2), face_jac.transpose(1, 2, 0, 3),
        jnp.asarray(sign_table()), jnp.asarray(low_mask()),
        block_inv.transpose(1, 2, 0, 3), trace, stiffness, lift,
    )
    return result.transpose(1, 0, 2)


def solution(mesh):
    return jax.shard_map(
        functools.partial(local, mesh.shape["dom"]),
        mesh=mesh,
        in_specs=(
            P("dom", None, None),
            P(),
            P("dom", None, None),
            P("dom", None, None, None),
            P("dom", None, None, None),
            P("dom", None),
            P("dom", None),
            P("dom", None),
            P("dom", None),
        ),
        out_specs=P("dom", None, None),
        check_vma=False,
    )
```

```python
import functools

import jax
import jax.numpy as jnp
import numpy as np
from jax import lax
from jax.experimental import pallas as pl
from jax.experimental.pallas import tpu as pltpu
from jax.sharding import PartitionSpec as P

QF = 8
QC = 4
SIGMA = 2.0
OMEGA = 0.7
SPAN = QF * QF
STEPS = 5
MESH = pl.DeviceIdType.MESH


def split_index(mode_id):
    return (mode_id // (QF * QF), mode_id // QF % QF, mode_id % QF)


def trace_table():
    matrix = np.zeros((QF**3, 6 * 2 * SPAN), np.float32)
    for mode_id in range(QF**3):
        triple = split_index(mode_id)
        for face_id in range(6):
            axis = face_id // 2
            a, b = [triple[place] for place in range(3) if place != axis]
            sign = (-1.0) ** triple[axis] if face_id % 2 == 0 else 1.0
            plain, turned = a * QF + b, b * QF + a
            low, high = (plain, turned) if face_id % 2 == 0 else (turned, plain)
            matrix[mode_id, face_id * 2 * SPAN + low] = sign
            matrix[mode_id, face_id * 2 * SPAN + SPAN + high] = sign
    return matrix


def lift_table():
    matrix = np.zeros((6 * SPAN, QF**3), np.float32)
    for mode_id in range(QF**3):
        triple = split_index(mode_id)
        for face_id in range(6):
            axis = face_id // 2
            a, b = [triple[place] for place in range(3) if place != axis]
            sign = (-1.0) ** triple[axis] if face_id % 2 == 0 else 1.0
            matrix[face_id * SPAN + a * QF + b, mode_id] = (2.0 * triple[axis] + 1.0) / 16.0 * sign
    return matrix


def sign_table():
    matrix = np.zeros((17, 16, 2 * SPAN), np.float32)
    for odd in range(2):
        for turn in range(8):
            half = (turn % 2) ^ odd
            for a in range(QF):
                for b in range(QF):
                    sign = 1.0
                    if turn // 2 % 2 == 1:
                        sign *= (-1.0) ** a
                    if turn // 4 % 2 == 1:
                        sign *= (-1.0) ** b
                    matrix[turn + 8 * odd, :, half * SPAN + a * QF + b] = sign
    return matrix


def low_mask():
    mask = np.zeros((8, QF**3), np.float32)
    for mode_id in range(QF**3):
        if max(split_index(mode_id)) < QC:
            mask[:, mode_id] = 1.0
    return mask


def halves(value):
    high = value.astype(jnp.bfloat16)
    return high, (value - high.astype(jnp.float32)).astype(jnp.bfloat16)


def kernel(
    n, elements, variables,
    owner_hbm, elem_hbm, side_hbm, turn_hbm, rhs_hbm, vol_hbm, face_hbm, signs_hbm, mask_hbm,
    inv_hbm, trace_hbm, stiff_hbm, lift_hbm,
    out,
    owner, elem, side_of, turn, rhs, vol, face, signs, mask,
    inv, inv_raw, trace, stiff, lift, stiff_hi, stiff_lo, jac_wide, vol_wide, small, jump, table,
    meta, request, asked_s, base_ref, now_ref, work_ref, kept_ref, coarse_ref, fine_ref,
    sent, got0, got1, got2, got3, got4,
    load_sem, ask_send, ask_recv, send_sem, recv_sem,
):
    got = (got0, got1, got2, got3, got4)
    me = lax.axis_index("dom")
    has = (me > 0, me < n - 1)
    other = (jnp.maximum(me - 1, 0), jnp.minimum(me + 1, n - 1))
    modes = rhs_hbm.shape[2]
    rows = elements * variables
    pairs = rows // 8
    half_reach = elements

    barrier = pltpu.get_barrier_semaphore()
    for side in range(2):
        @pl.when(has[side])
        def _():
            pl.semaphore_signal(barrier, inc=1, device_id=(other[side],), device_id_type=MESH)

    loads = {}
    for at, (name, source, target) in enumerate((
        ("owner", owner_hbm, owner), ("elem", elem_hbm, elem), ("side", side_hbm, side_of),
        ("turn", turn_hbm, turn), ("rhs", rhs_hbm, rhs), ("inv", inv_hbm, inv_raw),
        ("trace", trace_hbm, trace), ("stiff", stiff_hbm, stiff), ("vol", vol_hbm, vol),
        ("face", face_hbm, face), ("signs", signs_hbm, signs), ("mask", mask_hbm, mask),
        ("lift", lift_hbm, lift),
    )):
        loads[name] = pltpu.make_async_copy(source, target, load_sem.at[at])
        loads[name].start()
    for name in ("owner", "elem", "side", "turn"):
        loads[name].wait()

    spots = lax.broadcasted_iota(jnp.int32, (1, 128), 1)
    wanted = [jnp.zeros((1, 128), jnp.int32), jnp.zeros((1, 128), jnp.int32)]
    ranks = [jnp.int32(0), jnp.int32(0)]
    for e in range(elements):
        for f in range(6):
            at = e * 6 + f
            home = owner[e, f]
            face_turn, face_side, face_elem = turn[e, f], side_of[e, f], elem[e, f]
            present = home >= 0
            odd = face_side % 2
            swap = face_turn % 2
            half = (odd + swap) % 2
            tests = (present & (home == me - 1), present & (home == me + 1))
            for side in range(2):
                value = (face_elem * 6 + face_side) * 2 + half
                wanted[side] = jnp.where((spots == ranks[side]) & tests[side], value, wanted[side])
            rank = jnp.where(tests[1], ranks[1], ranks[0])
            far = tests[0] | tests[1]
            far_half = rank // half_reach
            meta[0, at] = jnp.where(tests[1], 1, 0)
            meta[1, at] = jnp.minimum(rank % half_reach, half_reach - 1)
            meta[2, at] = jnp.where(far, 1, 0)
            sign_row = face_turn + 8 * jnp.where(far, (far_half + swap) % 2, odd)
            meta[3, at] = jnp.where(present, sign_row, 16)
            for side in range(2):
                ranks[side] = ranks[side] + jnp.where(tests[side], 1, 0)
    request[0:1, :] = wanted[0]
    request[1:2, :] = wanted[1]

    pl.semaphore_wait(barrier, jnp.where(me > 0, 1, 0) + jnp.where(me < n - 1, 1, 0))

    def ask(side, slot):
        return pltpu.make_async_remote_copy(
            src_ref=request, dst_ref=asked_s.at[slot], send_sem=ask_send.at[side],
            recv_sem=ask_recv.at[slot], device_id=(other[side],), device_id_type=MESH,
        )

    for side in range(2):
        @pl.when(has[side])
        def _():
            ask(side, 1 - side).start()

    def twice(ref, w, lanes):
        row = ref[elements * w : elements * (w + 1), lanes]
        return jnp.concatenate([row, row], axis=0)

    def contract(wide, wide_lanes, source, c):
        lanes = slice(c * 128, (c + 1) * 128)
        totals = [None] * pairs
        for w in range(variables):
            row = twice(source, w, lanes)
            for p in range(pairs):
                term = wide[w, 8 * p : 8 * p + 8, wide_lanes] * row
                totals[p] = term if totals[p] is None else totals[p] + term
        return totals

    def smooth(source, width, emit):
        for c in range(width // 128):
            lanes = slice(c * 128, (c + 1) * 128)
            for p, total in enumerate(contract(inv, lanes, source, c)):
                emit(slice(8 * p, 8 * p + 8), lanes, OMEGA * total)

    loads["rhs"].wait()
    for v in range(variables):
        base_ref[elements * v : elements * (v + 1), :] = rhs[v]
    loads["inv"].wait()
    for v in range(variables):
        for w in range(variables):
            inv[w, elements * v : elements * (v + 1), :] = inv_raw[v, w]

    def first(at, lanes, value):
        now_ref[at, lanes] = value

    def following(at, lanes, value):
        now_ref[at, lanes] = now_ref[at, lanes] + value

    smooth(base_ref, modes, first)

    for side in range(2):
        @pl.when(has[side])
        def _():
            ask(side, side).wait()

    lane = lax.broadcasted_iota(jnp.int32, (variables, 2 * SPAN), 1)
    in_low = lane < SPAN

    def put(step, side, slot):
        return pltpu.make_async_remote_copy(
            src_ref=sent.at[step, side], dst_ref=got[step].at[slot], send_sem=send_sem.at[step, side],
            recv_sem=recv_sem.at[step, slot], device_id=(other[side],), device_id_type=MESH,
        )

    def face_load(place):
        return table[place % 6, pl.ds(place // 6, variables, stride=elements), :]

    def widen_jacobians():
        for f in range(6):
            for v in range(variables):
                small[f, elements * v : elements * (v + 1), :] = face[f, v]
        for v in range(variables):
            small[6, elements * v : elements * (v + 1), :] = vol[v]
        low8 = lax.broadcasted_iota(jnp.int32, (rows, 2 * SPAN), 1) < SPAN
        for w in range(variables):
            vol_wide[w] = jnp.broadcast_to(small[6, :, w : w + 1], (rows, 2 * SPAN))
            for pair in range(3):
                one = jnp.broadcast_to(small[2 * pair, :, w : w + 1], (rows, 2 * SPAN))
                two = jnp.broadcast_to(small[2 * pair + 1, :, w : w + 1], (rows, 2 * SPAN))
                jac_wide[w, :, pair * 2 * SPAN : (pair + 1) * 2 * SPAN] = jnp.where(low8, one, two)

    def residual(step, base, width_in, width_out, emit):
        value = now_ref[:, :width_in]
        high, low = halves(value)
        both = jnp.concatenate([high, low], axis=0)
        if step == 0:
            loads["trace"].wait()
        traced = jnp.dot(both, trace[:width_in, :], preferred_element_type=jnp.float32)
        traced = traced[:rows] + traced[rows:]
        for f in range(6):
            table[f] = traced[:, f * 2 * SPAN : (f + 1) * 2 * SPAN]
        for side in range(2):
            @pl.when(has[side])
            def _():
                for j in range(half_reach):
                    found = []
                    for half in range(2):
                        code = jnp.clip(asked_s[side, 1 - side, half * half_reach + j], 0, 12 * elements - 1)
                        piece = face_load(code // 2)
                        found.append(jnp.where(code % 2 == half, piece, pltpu.roll(piece, SPAN, axis=1)))
                    sent[step, side, j] = jnp.where(in_low, found[0], found[1])
                put(step, side, 1 - side).start()
        if step == 0:
            loads["stiff"].wait()
            stiff_high, stiff_low = halves(stiff[...])
            stiff_hi[...] = stiff_high
            stiff_lo[...] = stiff_low
            loads["vol"].wait()
            loads["face"].wait()
            widen_jacobians()
        blended = jnp.dot(both, stiff_hi[:width_in, :width_out], preferred_element_type=jnp.float32)
        blended = blended[:rows] + blended[rows:]
        blended = blended + jnp.dot(high, stiff_lo[:width_in, :width_out], preferred_element_type=jnp.float32)
        work_ref[:, :width_out] = blended
        for c in range(width_out // 128):
            lanes = slice(c * 128, (c + 1) * 128)
            for p, total in enumerate(contract(vol_wide, slice(0, 128), work_ref, c)):
                at = slice(8 * p, 8 * p + 8)
                kept_ref[at, lanes] = base[at, lanes] - SIGMA * now_ref[at, lanes] - total
        for side in range(2):
            @pl.when(has[side])
            def _():
                put(step, side, side).wait()
        if step == 0:
            loads["lift"].wait()
            loads["signs"].wait()
        for e in range(elements):
            for pair in range(3):
                faces = []
                for f in (2 * pair, 2 * pair + 1):
                    at = e * 6 + f
                    own = face_load(elem[e, f] * 6 + side_of[e, f])
                    far = got[step][meta[0, at], meta[1, at]]
                    picked = jnp.where(meta[2, at] > 0, far, own)
                    picked = picked * signs[meta[3, at]][:variables]
                    faces.append(picked + pltpu.roll(picked, SPAN, axis=1))
                at_e = pl.ds(e, variables, stride=elements)
                mine = jnp.where(in_low, table[2 * pair, at_e, :], table[2 * pair + 1, at_e, :])
                theirs = jnp.where(in_low, faces[0], faces[1])
                jump[pair, at_e, :] = mine - theirs
        columns = []
        for pair in range(3):
            lanes = slice(pair * 128, (pair + 1) * 128)
            columns.append(jnp.concatenate(contract(jac_wide, lanes, jump.at[pair], 0), axis=0))
        flux_high, flux_low = halves(jnp.concatenate(columns, axis=1))
        lifted = jnp.dot(
            jnp.concatenate([flux_high, flux_low], axis=0), lift[:, :width_out],
            preferred_element_type=jnp.float32,
        )
        emit(kept_ref[:, :width_out] - (lifted[:rows] + lifted[rows:]))

    short = QC * SPAN
    loads["mask"].wait()
    low_of = jnp.concatenate([mask[:, :short]] * pairs, axis=0)

    def to_work(value):
        work_ref[...] = value

    def to_coarse(value):
        coarse_ref[:, :short] = value * low_of

    def to_low_work(value):
        work_ref[:, :short] = value * low_of

    residual(0, base_ref, modes, modes, to_work)
    smooth(work_ref, modes, following)
    residual(1, base_ref, modes, short, to_coarse)
    fine_ref[...] = now_ref[...]
    smooth(coarse_ref, short, first)
    residual(2, coarse_ref, short, short, to_low_work)
    smooth(work_ref, short, following)
    now_ref[:, :short] = now_ref[:, :short] + fine_ref[:, :short]
    for step in (3, 4):
        residual(step, base_ref, modes, modes, to_work)
        smooth(work_ref, modes, following)
    for v in range(variables):
        out[v] = now_ref[elements * v : elements * (v + 1), :]


def local(n, rhs, stiffness, vol_jac, face_jac, block_inv, face_owner, face_elem, face_side, face_turn):
    elements, variables, modes = rhs.shape
    reach = 2 * elements
    trace = jnp.asarray(trace_table(), jnp.bfloat16)
    lift = jnp.asarray(lift_table(), jnp.bfloat16)
    signs, mask = jnp.asarray(sign_table()), jnp.asarray(low_mask())
    rows = elements * variables
    vmem = pl.BlockSpec(memory_space=pltpu.VMEM)
    hbm = pl.BlockSpec(memory_space=pltpu.HBM)
    f32, bf16, i32 = jnp.float32, jnp.bfloat16, jnp.int32
    dma = pltpu.SemaphoreType.DMA
    state = pltpu.VMEM((rows, modes), f32)
    result = pl.pallas_call(
        functools.partial(kernel, n, elements, variables),
        out_shape=jax.ShapeDtypeStruct((variables, elements, modes), f32),
        in_specs=[hbm] * 13,
        out_specs=vmem,
        scratch_shapes=[
            pltpu.SMEM(face_owner.shape, i32),
            pltpu.SMEM(face_owner.shape, i32),
            pltpu.SMEM(face_owner.shape, i32),
            pltpu.SMEM(face_owner.shape, i32),
            pltpu.VMEM((variables, elements, modes), f32),
            pltpu.VMEM((variables, elements, variables), f32),
            pltpu.VMEM((6, variables, elements, variables), f32),
            pltpu.VMEM(signs.shape, f32),
            pltpu.VMEM(mask.shape, f32),
            pltpu.VMEM((variables, rows, modes), f32),
            pltpu.VMEM((variables, variables, elements, modes), f32),
            pltpu.VMEM(trace.shape, bf16),
            pltpu.VMEM(stiffness.shape, f32),
            pltpu.VMEM(lift.shape, bf16),
            pltpu.VMEM(stiffness.shape, bf16),
            pltpu.VMEM(stiffness.shape, bf16),
            pltpu.VMEM((variables, rows, 6 * SPAN), f32),
            pltpu.VMEM((variables, rows, 2 * SPAN), f32),
            pltpu.VMEM((7, rows, variables), f32),
            pltpu.VMEM((3, rows, 2 * SPAN), f32),
            pltpu.VMEM((6, rows, 2 * SPAN), f32),
            pltpu.SMEM((4, 6 * elements), i32),
            pltpu.VMEM((8, 128), i32),
            pltpu.SMEM((2, 8, 128), i32),
            state, state, state, state, state, state,
            pltpu.VMEM((STEPS, 2, elements, variables, 2 * SPAN), f32),
        ] + [pltpu.VMEM((2, elements, variables, 2 * SPAN), f32)] * STEPS + [
            dma((13,)),
            dma((2,)),
            dma((2,)),
            dma((STEPS, 2)),
            dma((STEPS, 2)),
        ],
        compiler_params=pltpu.CompilerParams(
            collective_id=0, has_side_effects=True, vmem_limit_bytes=60 * 1024 * 1024
        ),
    )(
        face_owner, face_elem, face_side, face_turn,
        rhs.transpose(1, 0, 2), vol_jac.transpose(1, 0, 2), face_jac.transpose(1, 2, 0, 3),
        signs, mask,
        block_inv.transpose(1, 2, 0, 3), trace, stiffness, lift,
    )
    return result.transpose(1, 0, 2)


def solution(mesh):
    return jax.shard_map(
        functools.partial(local, mesh.shape["dom"]),
        mesh=mesh,
        in_specs=(
            P("dom", None, None),
            P(),
            P("dom", None, None),
            P("dom", None, None, None),
            P("dom", None, None, None),
            P("dom", None),
            P("dom", None),
            P("dom", None),
            P("dom", None),
        ),
        out_specs=P("dom", None, None),
        check_vma=False,
    )
```

```python
import functools

import jax
import jax.numpy as jnp
import numpy as np
from jax import lax
from jax.experimental import pallas as pl
from jax.experimental.pallas import tpu as pltpu
from jax.sharding import PartitionSpec as P

QF = 8
QC = 4
SIGMA = 2.0
OMEGA = 0.7
SPAN = QF * QF
STEPS = 5
MESH = pl.DeviceIdType.MESH


def split_index(mode_id):
    return (mode_id // (QF * QF), mode_id // QF % QF, mode_id % QF)


def trace_table():
    matrix = np.zeros((QF**3, 6 * 2 * SPAN), np.float32)
    for mode_id in range(QF**3):
        triple = split_index(mode_id)
        for face_id in range(6):
            axis = face_id // 2
            a, b = [triple[place] for place in range(3) if place != axis]
            sign = (-1.0) ** triple[axis] if face_id % 2 == 0 else 1.0
            plain, turned = a * QF + b, b * QF + a
            low, high = (plain, turned) if face_id % 2 == 0 else (turned, plain)
            matrix[mode_id, face_id * 2 * SPAN + low] = sign
            matrix[mode_id, face_id * 2 * SPAN + SPAN + high] = sign
    return matrix


def lift_table():
    matrix = np.zeros((6 * SPAN, QF**3), np.float32)
    for mode_id in range(QF**3):
        triple = split_index(mode_id)
        for face_id in range(6):
            axis = face_id // 2
            a, b = [triple[place] for place in range(3) if place != axis]
            sign = (-1.0) ** triple[axis] if face_id % 2 == 0 else 1.0
            matrix[face_id * SPAN + a * QF + b, mode_id] = (2.0 * triple[axis] + 1.0) / 16.0 * sign
    return matrix


def sign_table():
    matrix = np.zeros((17, 16, 2 * SPAN), np.float32)
    for odd in range(2):
        for turn in range(8):
            half = (turn % 2) ^ odd
            for a in range(QF):
                for b in range(QF):
                    sign = 1.0
                    if turn // 2 % 2 == 1:
                        sign *= (-1.0) ** a
                    if turn // 4 % 2 == 1:
                        sign *= (-1.0) ** b
                    matrix[turn + 8 * odd, :, half * SPAN + a * QF + b] = sign
    return matrix


def low_mask():
    mask = np.zeros((8, QF**3), np.float32)
    for mode_id in range(QF**3):
        if max(split_index(mode_id)) < QC:
            mask[:, mode_id] = 1.0
    return mask


def halves(value):
    high = value.astype(jnp.bfloat16)
    return high, (value - high.astype(jnp.float32)).astype(jnp.bfloat16)


def kernel(
    n, elements, variables,
    owner_hbm, elem_hbm, side_hbm, turn_hbm, rhs_hbm, vol_hbm, face_hbm, signs_hbm, mask_hbm,
    inv_hbm, trace_hbm, stiff_hbm, lift_hbm,
    out,
    owner, elem, side_of, turn, rhs, vol, face, signs, mask,
    inv, inv_raw, trace, stiff, lift, stiff_hi, stiff_lo, jac_wide, vol_wide, small, jump, table, whole,
    meta, request, asked_s, base_ref, now_ref, work_ref, kept_ref, coarse_ref, fine_ref,
    sent, got0, got1, got2, got3, got4,
    load_sem, ask_send, ask_recv, send_sem, recv_sem,
):
    got = (got0, got1, got2, got3, got4)
    me = lax.axis_index("dom")
    has = (me > 0, me < n - 1)
    other = (jnp.maximum(me - 1, 0), jnp.minimum(me + 1, n - 1))
    modes = rhs_hbm.shape[2]
    rows = elements * variables
    pairs = rows // 8
    half_reach = elements

    barrier = pltpu.get_barrier_semaphore()
    for side in range(2):
        @pl.when(has[side])
        def _():
            pl.semaphore_signal(barrier, inc=1, device_id=(other[side],), device_id_type=MESH)

    loads = {}
    for at, (name, source, target) in enumerate((
        ("owner", owner_hbm, owner), ("elem", elem_hbm, elem), ("side", side_hbm, side_of),
        ("turn", turn_hbm, turn), ("rhs", rhs_hbm, rhs), ("inv", inv_hbm, inv_raw),
        ("trace", trace_hbm, trace), ("stiff", stiff_hbm, stiff), ("vol", vol_hbm, vol),
        ("face", face_hbm, face), ("signs", signs_hbm, signs), ("mask", mask_hbm, mask),
        ("lift", lift_hbm, lift),
    )):
        loads[name] = pltpu.make_async_copy(source, target, load_sem.at[at])
        loads[name].start()
    for name in ("owner", "elem", "side", "turn"):
        loads[name].wait()

    spots = lax.broadcasted_iota(jnp.int32, (1, 128), 1)
    wanted = [jnp.zeros((1, 128), jnp.int32), jnp.zeros((1, 128), jnp.int32)]
    ranks = [jnp.int32(0), jnp.int32(0)]
    for e in range(elements):
        for f in range(6):
            at = e * 6 + f
            home = owner[e, f]
            face_turn, face_side, face_elem = turn[e, f], side_of[e, f], elem[e, f]
            present = home >= 0
            odd = face_side % 2
            swap = face_turn % 2
            half = (odd + swap) % 2
            tests = (present & (home == me - 1), present & (home == me + 1))
            for side in range(2):
                value = (face_elem * 6 + face_side) * 2 + half
                wanted[side] = jnp.where((spots == ranks[side]) & tests[side], value, wanted[side])
            rank = jnp.where(tests[1], ranks[1], ranks[0])
            far = tests[0] | tests[1]
            far_half = rank // half_reach
            meta[0, at] = jnp.where(tests[1], 1, 0)
            meta[1, at] = jnp.minimum(rank % half_reach, half_reach - 1)
            meta[2, at] = jnp.where(far, 1, 0)
            sign_row = face_turn + 8 * jnp.where(far, (far_half + swap) % 2, odd)
            meta[3, at] = jnp.where(present, sign_row, 16)
            meta[4, at] = jnp.where(present, face_turn + 8 * odd, 16)
            for side in range(2):
                ranks[side] = ranks[side] + jnp.where(tests[side], 1, 0)
    request[0:1, :] = wanted[0]
    request[1:2, :] = wanted[1]

    pl.semaphore_wait(barrier, jnp.where(me > 0, 1, 0) + jnp.where(me < n - 1, 1, 0))

    def ask(side, slot):
        return pltpu.make_async_remote_copy(
            src_ref=request, dst_ref=asked_s.at[slot], send_sem=ask_send.at[side],
            recv_sem=ask_recv.at[slot], device_id=(other[side],), device_id_type=MESH,
        )

    for side in range(2):
        @pl.when(has[side])
        def _():
            ask(side, 1 - side).start()

    def twice(ref, w, lanes):
        row = ref[elements * w : elements * (w + 1), lanes]
        return jnp.concatenate([row, row], axis=0)

    def contract(wide, wide_lanes, source, c):
        lanes = slice(c * 128, (c + 1) * 128)
        totals = [None] * pairs
        for w in range(variables):
            row = twice(source, w, lanes)
            for p in range(pairs):
                term = wide[w, 8 * p : 8 * p + 8, wide_lanes] * row
                totals[p] = term if totals[p] is None else totals[p] + term
        return totals

    def smooth(source, width, emit):
        for c in range(width // 128):
            lanes = slice(c * 128, (c + 1) * 128)
            for p, total in enumerate(contract(inv, lanes, source, c)):
                emit(slice(8 * p, 8 * p + 8), lanes, OMEGA * total)

    loads["rhs"].wait()
    for v in range(variables):
        base_ref[elements * v : elements * (v + 1), :] = rhs[v]
    loads["inv"].wait()
    for v in range(variables):
        for w in range(variables):
            inv[w, elements * v : elements * (v + 1), :] = inv_raw[v, w]

    def first(at, lanes, value):
        now_ref[at, lanes] = value

    def following(at, lanes, value):
        now_ref[at, lanes] = now_ref[at, lanes] + value

    smooth(base_ref, modes, first)


    lane = lax.broadcasted_iota(jnp.int32, (variables, 2 * SPAN), 1)
    in_low = lane < SPAN

    def put(step, side, slot):
        return pltpu.make_async_remote_copy(
            src_ref=whole if step == 0 else sent.at[step - 1, side], dst_ref=got[step].at[slot], send_sem=send_sem.at[step, side],
            recv_sem=recv_sem.at[step, slot], device_id=(other[side],), device_id_type=MESH,
        )

    def face_load(table, place):
        return table[place % 6, pl.ds(place // 6, variables, stride=elements), :]

    def widen_jacobians():
        for f in range(6):
            for v in range(variables):
                small[f, elements * v : elements * (v + 1), :] = face[f, v]
        for v in range(variables):
            small[6, elements * v : elements * (v + 1), :] = vol[v]
        low8 = lax.broadcasted_iota(jnp.int32, (rows, 2 * SPAN), 1) < SPAN
        for w in range(variables):
            vol_wide[w] = jnp.broadcast_to(small[6, :, w : w + 1], (rows, 2 * SPAN))
            for pair in range(3):
                one = jnp.broadcast_to(small[2 * pair, :, w : w + 1], (rows, 2 * SPAN))
                two = jnp.broadcast_to(small[2 * pair + 1, :, w : w + 1], (rows, 2 * SPAN))
                jac_wide[w, :, pair * 2 * SPAN : (pair + 1) * 2 * SPAN] = jnp.where(low8, one, two)

    def residual(step, base, width_in, width_out, emit):
        value = now_ref[:, :width_in]
        high, low = halves(value)
        both = jnp.concatenate([high, low], axis=0)
        tab = whole if step == 0 else table
        if step == 0:
            loads["trace"].wait()
        traced = jnp.dot(both, trace[:width_in, :], preferred_element_type=jnp.float32)
        traced = traced[:rows] + traced[rows:]
        for f in range(6):
            tab[f] = traced[:, f * 2 * SPAN : (f + 1) * 2 * SPAN]
        for side in range(2):
            @pl.when(has[side])
            def _():
                if step == 1:
                    ask(side, side).wait()
                for j in range(half_reach if step else 0):
                    found = []
                    for half in range(2):
                        code = jnp.clip(asked_s[side, 1 - side, half * half_reach + j], 0, 12 * elements - 1)
                        piece = face_load(tab, code // 2)
                        found.append(jnp.where(code % 2 == half, piece, pltpu.roll(piece, SPAN, axis=1)))
                    sent[step - 1, side, j] = jnp.where(in_low, found[0], found[1])
                put(step, side, 1 - side).start()
        if step == 0:
            loads["stiff"].wait()
            stiff_high, stiff_low = halves(stiff[...])
            stiff_hi[...] = stiff_high
            stiff_lo[...] = stiff_low
            loads["vol"].wait()
            loads["face"].wait()
            widen_jacobians()
        blended = jnp.dot(both, stiff_hi[:width_in, :width_out], preferred_element_type=jnp.float32)
        blended = blended[:rows] + blended[rows:]
        blended = blended + jnp.dot(high, stiff_lo[:width_in, :width_out], preferred_element_type=jnp.float32)
        work_ref[:, :width_out] = blended
        for c in range(width_out // 128):
            lanes = slice(c * 128, (c + 1) * 128)
            for p, total in enumerate(contract(vol_wide, slice(0, 128), work_ref, c)):
                at = slice(8 * p, 8 * p + 8)
                kept_ref[at, lanes] = base[at, lanes] - SIGMA * now_ref[at, lanes] - total
        for side in range(2):
            @pl.when(has[side])
            def _():
                put(step, side, side).wait()
        if step == 0:
            loads["lift"].wait()
            loads["signs"].wait()
        for e in range(elements):
            for pair in range(3):
                faces = []
                for f in (2 * pair, 2 * pair + 1):
                    at = e * 6 + f
                    place = elem[e, f] * 6 + side_of[e, f]
                    own = face_load(tab, place)
                    if step == 0:
                        far = face_load(got[0].at[meta[0, at]], place)
                    else:
                        far = got[step][meta[0, at], meta[1, at]]
                    picked = jnp.where(meta[2, at] > 0, far, own)
                    picked = picked * signs[meta[4 if step == 0 else 3, at]][:variables]
                    faces.append(picked + pltpu.roll(picked, SPAN, axis=1))
                at_e = pl.ds(e, variables, stride=elements)
                mine = jnp.where(in_low, tab[2 * pair, at_e, :], tab[2 * pair + 1, at_e, :])
                theirs = jnp.where(in_low, faces[0], faces[1])
                jump[pair, at_e, :] = mine - theirs
        columns = []
        for pair in range(3):
            lanes = slice(pair * 128, (pair + 1) * 128)
            columns.append(jnp.concatenate(contract(jac_wide, lanes, jump.at[pair], 0), axis=0))
        flux_high, flux_low = halves(jnp.concatenate(columns, axis=1))
        lifted = jnp.dot(
            jnp.concatenate([flux_high, flux_low], axis=0), lift[:, :width_out],
            preferred_element_type=jnp.float32,
        )
        emit(kept_ref[:, :width_out] - (lifted[:rows] + lifted[rows:]))

    short = QC * SPAN
    loads["mask"].wait()
    low_of = jnp.concatenate([mask[:, :short]] * pairs, axis=0)

    def to_work(value):
        work_ref[...] = value

    def to_coarse(value):
        coarse_ref[:, :short] = value * low_of

    def to_low_work(value):
        work_ref[:, :short] = value * low_of

    residual(0, base_ref, modes, modes, to_work)
    smooth(work_ref, modes, following)
    residual(1, base_ref, modes, short, to_coarse)
    fine_ref[...] = now_ref[...]
    smooth(coarse_ref, short, first)
    residual(2, coarse_ref, short, short, to_low_work)
    smooth(work_ref, short, following)
    now_ref[:, :short] = now_ref[:, :short] + fine_ref[:, :short]
    for step in (3, 4):
        residual(step, base_ref, modes, modes, to_work)
        smooth(work_ref, modes, following)
    for v in range(variables):
        out[v] = now_ref[elements * v : elements * (v + 1), :]


def local(n, rhs, stiffness, vol_jac, face_jac, block_inv, face_owner, face_elem, face_side, face_turn):
    elements, variables, modes = rhs.shape
    reach = 2 * elements
    trace = jnp.asarray(trace_table(), jnp.bfloat16)
    lift = jnp.asarray(lift_table(), jnp.bfloat16)
    signs, mask = jnp.asarray(sign_table()), jnp.asarray(low_mask())
    rows = elements * variables
    vmem = pl.BlockSpec(memory_space=pltpu.VMEM)
    hbm = pl.BlockSpec(memory_space=pltpu.HBM)
    f32, bf16, i32 = jnp.float32, jnp.bfloat16, jnp.int32
    dma = pltpu.SemaphoreType.DMA
    state = pltpu.VMEM((rows, modes), f32)
    result = pl.pallas_call(
        functools.partial(kernel, n, elements, variables),
        out_shape=jax.ShapeDtypeStruct((variables, elements, modes), f32),
        in_specs=[hbm] * 13,
        out_specs=vmem,
        scratch_shapes=[
            pltpu.SMEM(face_owner.shape, i32),
            pltpu.SMEM(face_owner.shape, i32),
            pltpu.SMEM(face_owner.shape, i32),
            pltpu.SMEM(face_owner.shape, i32),
            pltpu.VMEM((variables, elements, modes), f32),
            pltpu.VMEM((variables, elements, variables), f32),
            pltpu.VMEM((6, variables, elements, variables), f32),
            pltpu.VMEM(signs.shape, f32),
            pltpu.VMEM(mask.shape, f32),
            pltpu.VMEM((variables, rows, modes), f32),
            pltpu.VMEM((variables, variables, elements, modes), f32),
            pltpu.VMEM(trace.shape, bf16),
            pltpu.VMEM(stiffness.shape, f32),
            pltpu.VMEM(lift.shape, bf16),
            pltpu.VMEM(stiffness.shape, bf16),
            pltpu.VMEM(stiffness.shape, bf16),
            pltpu.VMEM((variables, rows, 6 * SPAN), f32),
            pltpu.VMEM((variables, rows, 2 * SPAN), f32),
            pltpu.VMEM((7, rows, variables), f32),
            pltpu.VMEM((3, rows, 2 * SPAN), f32),
            pltpu.VMEM((6, rows, 2 * SPAN), f32),
            pltpu.VMEM((6, rows, 2 * SPAN), f32),
            pltpu.SMEM((5, 6 * elements), i32),
            pltpu.VMEM((8, 128), i32),
            pltpu.SMEM((2, 8, 128), i32),
            state, state, state, state, state, state,
            pltpu.VMEM((STEPS - 1, 2, elements, variables, 2 * SPAN), f32),
            pltpu.VMEM((2, 6, rows, 2 * SPAN), f32),
        ] + [pltpu.VMEM((2, elements, variables, 2 * SPAN), f32)] * (STEPS - 1) + [
            dma((13,)),
            dma((2,)),
            dma((2,)),
            dma((STEPS, 2)),
            dma((STEPS, 2)),
        ],
        compiler_params=pltpu.CompilerParams(
            collective_id=0, has_side_effects=True, vmem_limit_bytes=40 * 1024 * 1024
        ),
    )(*[pltpu.with_memory_space_constraint(operand, pltpu.HBM) for operand in (
        face_owner, face_elem, face_side, face_turn,
        rhs.transpose(1, 0, 2), vol_jac.transpose(1, 0, 2), face_jac.transpose(1, 2, 0, 3),
        signs, mask, block_inv.transpose(1, 2, 0, 3), trace, stiffness, lift,
    )])
    return result.transpose(1, 0, 2)


def solution(mesh):
    return jax.shard_map(
        functools.partial(local, mesh.shape["dom"]),
        mesh=mesh,
        in_specs=(
            P("dom", None, None),
            P(),
            P("dom", None, None),
            P("dom", None, None, None),
            P("dom", None, None, None),
            P("dom", None),
            P("dom", None),
            P("dom", None),
            P("dom", None),
        ),
        out_specs=P("dom", None, None),
        check_vma=False,
    )
```
